32 devices in a mesh: groups: 2 (over y), fsdp: 4 (over x, core), tensor: 4 (over z).
Axes of the slice: x: 2, y: 2, z: 4, core: 2. Of those that a mesh axis runs over, the one named last changes fastest.
Arguments:
- tokens: bfloat16 [1024, 8192], P(('groups', 'fsdp')), parts along dimension 0, may hold values from -64 to 64
- gate_weight: bfloat16 [8192, 14336], P('fsdp', 'tensor'), may hold values from -0.0625 to 0.0625
- up_weight: bfloat16 [8192, 14336], P('fsdp', 'tensor'), may hold values from -0.0625 to 0.0625
- down_weight: bfloat16 [14336, 8192], P('tensor', 'fsdp'), may hold values from -0.046875 to 0.046875
- right_factor: bfloat16 [64, 128, 128], P('fsdp', 'tensor'), may hold values from -0.5 to 0.5
- left_factor: bfloat16 [128, 64, 64], P('fsdp', 'tensor'), may hold values from -0.75 to 0.75
Outputs:
- grad_right: float32 [128, 128, 128], P(('groups', 'fsdp'), 'tensor'), parts along dimension 0
- grad_left: float32 [256, 64, 64], P(('groups', 'fsdp'), 'tensor'), parts along dimension 0
The draws below stay inside these ranges and needn't reach their ends.
There are 2 independent parts, one for each index of `groups`. The reference program is written for one: setup_inputs(seed, part) draws one part's arguments, and reference() takes and returns one part's arrays. A program takes and returns all parts, laid end to end along the dimension named above; an argument that names none is the same for every part. Nothing has to cross between parts.
All inputs are finite; a program needn't handle non-finite values.
Results may differ from the reference program's by a relative error of at most 0.0055.
Values may be sent and summed in bfloat16 or wider, within the bound.
A program may use at most 128 MiB of HBM per device.

```python
import math
import jax
import jax.numpy as jnp
from jax import lax

D = 8192
FF = 14336
NBLK = 64
BSZ = 128
TOKENS = 512
FEAT_SHARE = 2048
HIDDEN_SHARE = 3584


def draw_tokens(key, part):
    base_key, row_key, col_key = jax.random.split(jax.random.fold_in(key, 11), 3)
    base = jnp.clip(jax.random.normal(base_key, (TOKENS, D), jnp.float32), -6.0, 6.0)
    row_scale = jnp.exp(jax.random.uniform(row_key, (TOKENS, 1), jnp.float32, -0.1, 0.1))
    col_scale = 0.6 * jnp.exp(jax.random.uniform(col_key, (1, D), jnp.float32, -1.15, 1.15))
    return (base * row_scale * col_scale).astype(jnp.bfloat16)


def levels(stream_key, shape, pieces, smallest, top_value):
    loudness, own = 1.0, jax.random.fold_in(stream_key, 6)
    for position, blocks in pieces:
        draws = jnp.exp(jax.random.uniform(jax.random.fold_in(own, position), (blocks,), jnp.float32, smallest / len(pieces), top_value / len(pieces)))
        loudness = loudness * jnp.repeat(draws, shape[position] // blocks).reshape([-1 if axis == position else 1 for axis in range(len(shape))])
    return loudness


def centred(own_key, extent, spread, limit, cuts=(), dtype=jnp.bfloat16):
    factor_of = levels(own_key, extent, cuts, -0.22, 0.18) if cuts else 1.0
    array = jax.random.normal(own_key, extent, jnp.float32) * spread * factor_of
    return jnp.minimum(jnp.maximum(array, -limit), limit).astype(dtype)


def setup_inputs(seed: int = 0, part: int = 0) -> dict:
    splits = jax.random.split(jax.random.key(seed), 7)
    part_keys = jax.random.split(jax.random.fold_in(splits[6], part), 7)
    tokens = draw_tokens(jax.random.fold_in(jax.random.fold_in(splits[6], part), 71), part)
    gate_weight = centred(splits[1], (D, FF), D ** -0.5, 0.0625, ((0, 4), (1, 4)))
    up_weight = centred(splits[2], (D, FF), D ** -0.5, 0.0625, ((0, 4), (1, 4)))
    down_weight = centred(splits[3], (FF, D), FF ** -0.5, 0.046875, ((0, 4), (1, 4)))
    right_factor = centred(splits[4], (NBLK, BSZ, BSZ), BSZ ** -0.5, 0.5, ((0, 4), (1, 4)))
    left_factor = centred(splits[5], (BSZ, NBLK, NBLK), NBLK ** -0.5, 0.75, ((0, 4), (1, 4)))
    return dict(tokens=tokens, gate_weight=gate_weight, up_weight=up_weight, down_weight=down_weight, right_factor=right_factor, left_factor=left_factor)


def grouped_product(left_parts, right_parts, rows, width):

    def add_group(total, pair):
        product = jnp.dot(pair[0], pair[1], preferred_element_type=jnp.float32)
        rounded = lax.optimization_barrier(product.astype(jnp.bfloat16))
        return (total + rounded.astype(jnp.float32), None)
    start = jnp.zeros((rows, width), jnp.float32)
    return lax.scan(add_group, start, (left_parts, right_parts))[0]

def reference(tokens, gate_weight, up_weight, down_weight, right_factor, left_factor):
    feature_groups = D // FEAT_SHARE
    hidden_groups = FF // HIDDEN_SHARE
    token_parts = jnp.moveaxis(tokens.reshape(TOKENS, feature_groups, FEAT_SHARE), 1, 0)
    gate_sum = grouped_product(token_parts, gate_weight.reshape(feature_groups, FEAT_SHARE, FF), TOKENS, FF)
    up_sum = grouped_product(token_parts, up_weight.reshape(feature_groups, FEAT_SHARE, FF), TOKENS, FF)
    hidden = (jax.nn.silu(gate_sum) * up_sum).astype(jnp.bfloat16)
    hidden_parts = jnp.moveaxis(hidden.reshape(TOKENS, hidden_groups, HIDDEN_SHARE), 1, 0)
    target = grouped_product(hidden_parts, down_weight.reshape(hidden_groups, HIDDEN_SHARE, D), TOKENS, D)
    block_input = tokens.reshape(TOKENS, NBLK, BSZ).astype(jnp.float32)
    mixed = jnp.einsum('nij,ikj->nik', block_input, right_factor.astype(jnp.float32)).astype(jnp.bfloat16)
    left_wide = left_factor.astype(jnp.float32)
    mixed_wide = mixed.astype(jnp.float32)
    student = jnp.einsum('nij,jki->njk', mixed_wide, left_wide)
    out_grad = (student - target.reshape(TOKENS, BSZ, NBLK)) / math.sqrt(TOKENS)
    grad_left = jnp.einsum('njk,nij->jki', out_grad, mixed_wide)
    mixed_grad = jnp.einsum('njk,jki->nij', out_grad, left_wide).astype(jnp.bfloat16)
    grad_right = jnp.einsum('nik,nij->ikj', mixed_grad.astype(jnp.float32), block_input)
    return (grad_right, grad_left)
```

```python
import functools
import math

import jax
import jax.numpy as jnp
from jax import lax
from jax.experimental import pallas as pl
from jax.experimental.pallas import tpu as pltpu
from jax.sharding import PartitionSpec as P

MESH = pl.DeviceIdType.MESH
CHUNK = 512
PIECES = 4


def plain_body(tokens, gate_weight, up_weight, down_weight, right_factor, left_factor):
    fsdp_count = lax.axis_size("fsdp")
    tensor_count = lax.axis_size("tensor")
    tok_local = tokens.shape[0]
    group_rows = tok_local * fsdp_count
    share_rows = group_rows // tensor_count
    hid_local = gate_weight.shape[1]
    spread = lax.all_to_all(tokens, "fsdp", split_axis=1, concat_axis=0, tiled=True)
    student_in = lax.dynamic_slice_in_dim(
        spread, lax.axis_index("tensor") * share_rows, share_rows, 0
    )
    gate_part = jnp.dot(spread, gate_weight, preferred_element_type=jnp.float32)
    up_part = jnp.dot(spread, up_weight, preferred_element_type=jnp.float32)
    partial_value = jnp.concatenate([gate_part, up_part], axis=1)
    summed = lax.psum(partial_value.astype(jnp.bfloat16), "fsdp").astype(jnp.float32)
    hidden = (jax.nn.silu(summed[:, :hid_local]) * summed[:, hid_local:]).astype(jnp.bfloat16)
    target = lax.psum_scatter(
        jnp.dot(hidden, down_weight, preferred_element_type=jnp.float32).astype(jnp.bfloat16),
        "tensor",
        scatter_dimension=0,
        tiled=True,
    ).astype(jnp.float32)
    right_full, left_full = (
        lax.all_gather(right_factor, "tensor", axis=1, tiled=True),
        lax.all_gather(left_factor, "tensor", axis=1, tiled=True),
    )
    blocks_local = right_full.shape[0]
    block_size = right_full.shape[2]
    block_input = student_in.reshape(share_rows, blocks_local, block_size)
    mixed = jnp.einsum(
        "nij,ikj->nik", block_input, right_full, preferred_element_type=jnp.float32
    ).astype(jnp.bfloat16)
    routed = lax.all_to_all(mixed, "fsdp", split_axis=2, concat_axis=1, tiled=True)
    student = jnp.einsum("nij,jki->njk", routed, left_full, preferred_element_type=jnp.float32)
    inv_root = 1.0 / math.sqrt(group_rows)
    out_grad = (student - target.reshape(student.shape)) * inv_root
    grad_left = jnp.einsum("njk,nij->jki", out_grad, routed.astype(jnp.float32))
    mixed_grad = jnp.einsum("njk,jki->nij", out_grad, left_full.astype(jnp.float32)).astype(
        jnp.bfloat16
    )
    returned = lax.all_to_all(mixed_grad, "fsdp", split_axis=1, concat_axis=2, tiled=True)
    grad_right = jnp.einsum(
        "nik,nij->ikj", returned.astype(jnp.float32), block_input.astype(jnp.float32)
    )
    grad_right, grad_left = (
        lax.psum_scatter(grad_right, "tensor", scatter_dimension=1, tiled=True),
        lax.psum_scatter(grad_left, "tensor", scatter_dimension=1, tiled=True),
    )
    return (grad_right, grad_left)


def teacher_kernel(
    n, T, rows, width, cols,
    tok, gw, uw, dw, spread, tgt,
    wg, wu, wd, pbuf, recv_a, sbuf, recv_b, hid, acc, send_z, recv_z,
    tok_send, tok_recv, w_sem, a_send, a_recv, b_send, b_recv,
    hx_send, hx_recv, hp_send, hp_recv, r_send, r_recv, z_send, z_recv,
):
    f32, bf16 = jnp.float32, jnp.bfloat16
    f = lax.axis_index("fsdp")
    z = lax.axis_index("tensor")
    x, c = f // 2, f % 2
    partner = x * 2 + (1 - c)
    across = (1 - x) * 2 + c
    diag = (1 - x) * 2 + (1 - c)
    q = c * 2 + x
    q_across = c * 2 + (1 - x)
    features = spread.shape[2]

    def weights(t):
        s = lax.rem(t, 2)
        cc = pl.ds(pl.multiple_of(t * width, width), width)
        return (
            pltpu.make_async_copy(gw.at[:, cc], wg.at[s], w_sem.at[0, s]),
            pltpu.make_async_copy(uw.at[:, cc], wu.at[s], w_sem.at[1, s]),
        )

    def down(t):
        s = lax.rem(t, 2)
        return pltpu.make_async_copy(
            dw.at[pl.ds(pl.multiple_of(t * width, width), width), :], wd.at[s], w_sem.at[2, s]
        )

    for cp in weights(0):
        cp.start()
    down(0).start()

    barrier = pltpu.get_barrier_semaphore()
    for peer in (partner, across, diag):
        pl.semaphore_signal(barrier, inc=1, device_id={"fsdp": peer}, device_id_type=MESH)

    @pl.when(z > 0)
    def _():
        pl.semaphore_signal(barrier, inc=1, device_id={"tensor": z - 1}, device_id_type=MESH)

    @pl.when(z < T - 1)
    def _():
        pl.semaphore_signal(barrier, inc=1, device_id={"tensor": z + 1}, device_id_type=MESH)

    pl.semaphore_wait(barrier, 3 + (z + T - 1) // T + (2 * T - 2 - z) // T)

    def tok_copy(i, peer):
        cc = pl.ds(pl.multiple_of(peer * features, features), features)
        return pltpu.make_async_remote_copy(
            tok.at[:, cc], spread.at[q], tok_send.at[i], tok_recv.at[i],
            device_id={"fsdp": peer}, device_id_type=MESH,
        )

    exchange = [tok_copy(0, across), tok_copy(1, diag), tok_copy(2, partner)]
    for cp in exchange:
        cp.start()
    own = pltpu.make_async_copy(
        tok.at[:, pl.ds(pl.multiple_of(f * features, features), features)],
        spread.at[q], tok_send.at[3],
    )
    own.start()
    acc[...] = jnp.zeros_like(acc)
    own.wait()
    for cp in exchange:
        cp.wait()

    def send_a(t):
        return pltpu.make_async_remote_copy(
            pbuf.at[t, 1 - c], recv_a.at[t], a_send.at[t], a_recv.at[t],
            device_id={"fsdp": partner}, device_id_type=MESH)

    def send_b(t):
        return pltpu.make_async_remote_copy(
            sbuf.at[t, 1 - x], recv_b.at[t], b_send.at[t], b_recv.at[t],
            device_id={"fsdp": across}, device_id_type=MESH)

    def send_hx(t):
        return pltpu.make_async_remote_copy(
            hid.at[t, q], hid.at[t, q], hx_send.at[t], hx_recv.at[t],
            device_id={"fsdp": across}, device_id_type=MESH)

    def send_hp(t):
        return pltpu.make_async_remote_copy(
            hid.at[t, q], hid.at[t, q], hp_send.at[t], hp_recv.at[t],
            device_id={"fsdp": partner}, device_id_type=MESH)

    def send_r(t):
        return pltpu.make_async_remote_copy(
            hid.at[t, q_across], hid.at[t, q_across], r_send.at[t], r_recv.at[t],
            device_id={"fsdp": partner}, device_id_type=MESH)

    def step(t, carry):
        @pl.when(t < n)
        def _():
            @pl.when(t + 1 < n)
            def _():
                for cp in weights(t + 1):
                    cp.start()

            for cp in weights(t):
                cp.wait()
            s = lax.rem(t, 2)
            toks = spread[...].reshape(4 * rows, features)
            for k, w in ((0, wg), (1, wu)):
                part = jnp.dot(toks, w[s], preferred_element_type=f32).astype(bf16)
                for h in range(2):
                    pbuf[t, h, k] = part[h * 2 * rows:(h + 1) * 2 * rows]
            send_a(t).start()

        @pl.when(t >= 3)
        def _():
            u = t - 3

            @pl.when(u + 1 < n)
            def _():
                down(u + 1).start()

            down(u).wait()
            send_hp(u).wait_recv()
            send_r(u).wait_recv()
            s = lax.rem(u, 2)
            h = hid[u].reshape(4 * rows, width)

            @pl.loop(0, T)
            def _(b):
                cc = pl.ds(pl.multiple_of(b * cols, cols), cols)
                acc[b] += jnp.dot(h, wd[s, :, cc], preferred_element_type=f32)

        @pl.when(t < n)
        def _():
            send_a(t).wait_recv()
            for k in range(2):
                total = pbuf[t, c, k].astype(f32) + recv_a[t, k].astype(f32)
                total = total.astype(bf16)
                for h in range(2):
                    sbuf[t, h, k] = total[h * rows:(h + 1) * rows]
            send_b(t).start()

        @pl.when((t >= 1) & (t < n + 1))
        def _():
            u = t - 1
            send_b(u).wait_recv()
            gate = sbuf[u, x, 0].astype(f32) + recv_b[u, 0].astype(f32)
            up = sbuf[u, x, 1].astype(f32) + recv_b[u, 1].astype(f32)
            hid[u, q] = (jax.nn.silu(gate) * up).astype(bf16)
            send_hx(u).start()
            send_hp(u).start()

        @pl.when((t >= 2) & (t < n + 2))
        def _():
            u = t - 2
            send_hx(u).wait_recv()
            send_r(u).start()

        return carry

    lax.fori_loop(0, n + 3, step, 0)

    piece = 4 * rows // PIECES

    def send_right(d, s):
        return pltpu.make_async_remote_copy(
            send_z.at[0, d, s], recv_z.at[0, d, s], z_send.at[0, d, s], z_recv.at[0, d, s],
            device_id={"tensor": z + 1}, device_id_type=MESH)

    def send_left(d, s):
        return pltpu.make_async_remote_copy(
            send_z.at[1, d, s], recv_z.at[1, d, s], z_send.at[1, d, s], z_recv.at[1, d, s],
            device_id={"tensor": z - 1}, device_id_type=MESH)

    def hop(way, d, s, has_prev, sender):
        rr = slice(s * piece, (s + 1) * piece)
        mine = acc[d, rr].astype(bf16)
        send_z[way, d, s] = mine

        @pl.when(has_prev)
        def _():
            sender(d, s).wait_recv()
            send_z[way, d, s] = (mine.astype(f32) + recv_z[way, d, s].astype(f32)).astype(bf16)

        sender(d, s).start()

    for j in range(T - 1):
        for s in range(PIECES):
            dr, dl = T - 1 - j, j

            @pl.when(z < dr)
            def _():
                hop(0, dr, s, z > 0, send_right)

            @pl.when(z > dl)
            def _():
                hop(1, dl, s, z < T - 1, send_left)

    for s in range(PIECES):
        rr = slice(s * piece, (s + 1) * piece)
        tgt[rr] = acc[z, rr].astype(bf16).astype(f32)

        @pl.when(z > 0)
        def _():
            send_right(z, s).wait_recv()
            tgt[rr] += recv_z[0, z, s].astype(f32)

        @pl.when(z < T - 1)
        def _():
            send_left(z, s).wait_recv()
            tgt[rr] += recv_z[1, z, s].astype(f32)

    for j in range(T - 1):
        for s in range(PIECES):
            dr, dl = T - 1 - j, j

            @pl.when(z < dr)
            def _():
                send_right(dr, s).wait_send()

            @pl.when(z > dl)
            def _():
                send_left(dl, s).wait_send()

    def drain(t, carry):
        for sender in (send_a, send_b, send_hx, send_hp, send_r):
            sender(t).wait_send()
        return carry

    lax.fori_loop(0, n, drain, 0)


def teacher(tokens, gate_weight, up_weight, down_weight, T):
    rows = tokens.shape[0]
    features, hidden = gate_weight.shape
    width = CHUNK
    n = hidden // width
    cols = down_weight.shape[1] // T
    bf16, f32 = jnp.bfloat16, jnp.float32
    dma = pltpu.SemaphoreType.DMA
    anyspace = pl.BlockSpec(memory_space=pl.ANY)
    vmem = pl.BlockSpec(memory_space=pltpu.VMEM)
    return pl.pallas_call(
        functools.partial(teacher_kernel, n, T, rows, width, cols),
        out_shape=(
            jax.ShapeDtypeStruct((4, rows, features), bf16),
            jax.ShapeDtypeStruct((4 * rows, cols), f32),
        ),
        in_specs=[anyspace] * 4,
        out_specs=(vmem, vmem),
        scratch_shapes=[
            pltpu.VMEM((2, features, width), bf16),
            pltpu.VMEM((2, features, width), bf16),
            pltpu.VMEM((2, width, T * cols), bf16),
            pltpu.VMEM((n, 2, 2, 2 * rows, width), bf16),
            pltpu.VMEM((n, 2, 2 * rows, width), bf16),
            pltpu.VMEM((n, 2, 2, rows, width), bf16),
            pltpu.VMEM((n, 2, rows, width), bf16),
            pltpu.VMEM((n, 4, rows, width), bf16),
            pltpu.VMEM((T, 4 * rows, cols), f32),
            pltpu.VMEM((2, T, PIECES, 4 * rows // PIECES, cols), bf16),
            pltpu.VMEM((2, T, PIECES, 4 * rows // PIECES, cols), bf16),
            dma((4,)), dma((3,)), dma((3, 2)),
            dma((n,)), dma((n,)), dma((n,)), dma((n,)),
            dma((n,)), dma((n,)), dma((n,)), dma((n,)), dma((n,)), dma((n,)),
            dma((2, T, PIECES)), dma((2, T, PIECES)),
        ],
        compiler_params=pltpu.CompilerParams(
            collective_id=0, has_side_effects=True, vmem_limit_bytes=62 * 1024 * 1024
        ),
        name="teacher",
    )(tokens, gate_weight, up_weight, down_weight)


def fused_body(tokens, gate_weight, up_weight, down_weight, right_factor, left_factor):
    T = lax.axis_size("tensor")
    rows = tokens.shape[0] * lax.axis_size("fsdp")
    right = lax.all_to_all(right_factor, "tensor", split_axis=1, concat_axis=1, tiled=True)
    left = lax.all_to_all(left_factor, "tensor", split_axis=0, concat_axis=1, tiled=True)
    spread, target = teacher(tokens, gate_weight, up_weight, down_weight, T)
    blocks, size = right.shape[0], right.shape[2]
    block_input = spread.reshape(rows, blocks, size)
    mixed = jnp.einsum(
        "nij,ikj->nik", block_input, right, preferred_element_type=jnp.float32
    ).astype(jnp.bfloat16)
    routed = lax.all_to_all(mixed, "fsdp", split_axis=2, concat_axis=1, tiled=True)
    student = jnp.einsum("nij,jki->njk", routed, left, preferred_element_type=jnp.float32)
    out_grad = (student - target.reshape(student.shape)) * (1.0 / math.sqrt(rows))
    grad_left = jnp.einsum("njk,nij->jki", out_grad, routed.astype(jnp.float32))
    mixed_grad = jnp.einsum("njk,jki->nij", out_grad, left.astype(jnp.float32)).astype(
        jnp.bfloat16
    )
    returned = lax.all_to_all(mixed_grad, "fsdp", split_axis=1, concat_axis=2, tiled=True)
    grad_right = jnp.einsum(
        "nik,nij->ikj", returned.astype(jnp.float32), block_input.astype(jnp.float32)
    )
    grad_right = lax.all_to_all(grad_right, "tensor", split_axis=1, concat_axis=1, tiled=True)
    grad_left = lax.all_to_all(grad_left, "tensor", split_axis=1, concat_axis=0, tiled=True)
    return (grad_right, grad_left)


def body(tokens, gate_weight, up_weight, down_weight, right_factor, left_factor):
    F, T = lax.axis_size("fsdp"), lax.axis_size("tensor")
    fits = (
        F == 4
        and T == 4
        and gate_weight.shape[1] % CHUNK == 0
        and left_factor.shape[0] % T == 0
        and right_factor.shape[1] % T == 0
        and gate_weight.shape[0] <= 2048
        and tokens.shape[0] == 128
    )
    run = fused_body if fits else plain_body
    return run(tokens, gate_weight, up_weight, down_weight, right_factor, left_factor)


def solution(mesh):
    return jax.shard_map(
        body,
        mesh=mesh,
        in_specs=(
            P(("groups", "fsdp"), None),
            P("fsdp", "tensor"),
            P("fsdp", "tensor"),
            P("tensor", "fsdp"),
            P("fsdp", "tensor", None),
            P("fsdp", "tensor", None),
        ),
        out_specs=(P(("groups", "fsdp"), "tensor", None), P(("groups", "fsdp"), "tensor", None)),
        check_vma=False,
    )
```

```python
import functools
import math

import jax
import jax.numpy as jnp
from jax import lax
from jax.experimental import pallas as pl
from jax.experimental.pallas import tpu as pltpu
from jax.sharding import PartitionSpec as P

MESH = pl.DeviceIdType.MESH
CHUNK = 512
PIECES = 4


def plain_body(tokens, gate_weight, up_weight, down_weight, right_factor, left_factor):
    fsdp_count = lax.axis_size("fsdp")
    tensor_count = lax.axis_size("tensor")
    tok_local = tokens.shape[0]
    group_rows = tok_local * fsdp_count
    share_rows = group_rows // tensor_count
    hid_local = gate_weight.shape[1]
    spread = lax.all_to_all(tokens, "fsdp", split_axis=1, concat_axis=0, tiled=True)
    student_in = lax.dynamic_slice_in_dim(
        spread, lax.axis_index("tensor") * share_rows, share_rows, 0
    )
    gate_part = jnp.dot(spread, gate_weight, preferred_element_type=jnp.float32)
    up_part = jnp.dot(spread, up_weight, preferred_element_type=jnp.float32)
    partial_value = jnp.concatenate([gate_part, up_part], axis=1)
    summed = lax.psum(partial_value.astype(jnp.bfloat16), "fsdp").astype(jnp.float32)
    hidden = (jax.nn.silu(summed[:, :hid_local]) * summed[:, hid_local:]).astype(jnp.bfloat16)
    target = lax.psum_scatter(
        jnp.dot(hidden, down_weight, preferred_element_type=jnp.float32).astype(jnp.bfloat16),
        "tensor",
        scatter_dimension=0,
        tiled=True,
    ).astype(jnp.float32)
    right_full, left_full = (
        lax.all_gather(right_factor, "tensor", axis=1, tiled=True),
        lax.all_gather(left_factor, "tensor", axis=1, tiled=True),
    )
    blocks_local = right_full.shape[0]
    block_size = right_full.shape[2]
    block_input = student_in.reshape(share_rows, blocks_local, block_size)
    mixed = jnp.einsum(
        "nij,ikj->nik", block_input, right_full, preferred_element_type=jnp.float32
    ).astype(jnp.bfloat16)
    routed = lax.all_to_all(mixed, "fsdp", split_axis=2, concat_axis=1, tiled=True)
    student = jnp.einsum("nij,jki->njk", routed, left_full, preferred_element_type=jnp.float32)
    inv_root = 1.0 / math.sqrt(group_rows)
    out_grad = (student - target.reshape(student.shape)) * inv_root
    grad_left = jnp.einsum("njk,nij->jki", out_grad, routed.astype(jnp.float32))
    mixed_grad = jnp.einsum("njk,jki->nij", out_grad, left_full.astype(jnp.float32)).astype(
        jnp.bfloat16
    )
    returned = lax.all_to_all(mixed_grad, "fsdp", split_axis=1, concat_axis=2, tiled=True)
    grad_right = jnp.einsum(
        "nik,nij->ikj", returned.astype(jnp.float32), block_input.astype(jnp.float32)
    )
    grad_right, grad_left = (
        lax.psum_scatter(grad_right, "tensor", scatter_dimension=1, tiled=True),
        lax.psum_scatter(grad_left, "tensor", scatter_dimension=1, tiled=True),
    )
    return (grad_right, grad_left)


def layer_kernel(
    n, T, rows, width, cols,
    tok, gw, uw, dw, right, left, gr_out, gl_out,
    wg, wu, wd, pbuf, recv_a, sbuf, recv_b, hid, acc, send_z, recv_z,
    spread, tgt, rki, lji, rbig, lbig, mix_s, routed, student, mg_s, mg_r, gr_s, gl_s,
    tok_send, tok_recv, w_sem, a_send, a_recv, b_send, b_recv,
    hx_send, hx_recv, hp_send, hp_recv, r_send, r_recv, z_send, z_recv,
    rf_send, rf_recv, lf_send, lf_recv, mix_send, mix_recv, mg_send, mg_recv,
    gr_send, gr_recv, gl_send, gl_recv,
):
    f32, bf16 = jnp.float32, jnp.bfloat16
    f = lax.axis_index("fsdp")
    z = lax.axis_index("tensor")
    x, c = f // 2, f % 2
    partner = x * 2 + (1 - c)
    across = (1 - x) * 2 + c
    diag = (1 - x) * 2 + (1 - c)
    q = c * 2 + x
    q_across = c * 2 + (1 - x)
    features = spread.shape[2]

    def weights(t):
        s = lax.rem(t, 2)
        cc = pl.ds(pl.multiple_of(t * width, width), width)
        return (
            pltpu.make_async_copy(gw.at[:, cc], wg.at[s], w_sem.at[0, s]),
            pltpu.make_async_copy(uw.at[:, cc], wu.at[s], w_sem.at[1, s]),
        )

    def down(t):
        s = lax.rem(t, 2)
        return pltpu.make_async_copy(
            dw.at[pl.ds(pl.multiple_of(t * width, width), width), :], wd.at[s], w_sem.at[2, s]
        )

    for cp in weights(0):
        cp.start()
    down(0).start()

    barrier = pltpu.get_barrier_semaphore()
    for peer in (partner, across, diag):
        pl.semaphore_signal(barrier, inc=1, device_id={"fsdp": peer}, device_id_type=MESH)

    for d in range(1, T):
        pl.semaphore_signal(
            barrier, inc=1, device_id={"tensor": lax.rem(z + d, T)}, device_id_type=MESH)
    pl.semaphore_wait(barrier, 3 + T - 1)

    def tok_copy(i, peer):
        cc = pl.ds(pl.multiple_of(peer * features, features), features)
        return pltpu.make_async_remote_copy(
            tok.at[:, cc], spread.at[q], tok_send.at[i], tok_recv.at[i],
            device_id={"fsdp": peer}, device_id_type=MESH,
        )

    exchange = [tok_copy(0, across), tok_copy(1, diag), tok_copy(2, partner)]
    for cp in exchange:
        cp.start()
    own = pltpu.make_async_copy(
        tok.at[:, pl.ds(pl.multiple_of(f * features, features), features)],
        spread.at[q], tok_send.at[3],
    )
    own.start()
    acc[...] = jnp.zeros_like(acc)

    N = 4 * rows
    na, ni, nj = rki.shape[1:]
    nk, nf = lji.shape[2] * T, na * ni
    nb = lji.shape[3]

    def right_copy(d):
        peer = lax.rem(z + d, T)
        return pltpu.make_async_remote_copy(
            right.at[pl.ds(peer * na, na)], rki.at[z], rf_send.at[d], rf_recv.at[d],
            device_id={"tensor": peer}, device_id_type=MESH)

    def left_copy(d):
        peer = lax.rem(z + d, T)
        return pltpu.make_async_remote_copy(
            left.at[pl.ds(peer * na, na)], lji.at[:, z], lf_send.at[d], lf_recv.at[d],
            device_id={"tensor": peer}, device_id_type=MESH)

    factors = [right_copy(d) for d in range(1, T)] + [left_copy(d) for d in range(1, T)]
    for cp in factors:
        cp.start()
    own_right = pltpu.make_async_copy(right.at[pl.ds(z * na, na)], rki.at[z], rf_send.at[0])
    own_left = pltpu.make_async_copy(left.at[pl.ds(z * na, na)], lji.at[:, z], lf_send.at[0])
    own_right.start()
    own_left.start()
    own_right.wait()
    own_left.wait()
    for cp in factors:
        cp.wait()

    iota = functools.partial(lax.broadcasted_iota, jnp.int32)
    packed = rki[...].reshape(T * nf, nj)
    lane_block = lax.rem(iota((T * nf, nj), 0), ni)
    for i in range(ni):
        rbig[:, i * nj:(i + 1) * nj] = jnp.where(lane_block == i, packed, jnp.zeros_like(packed))
    col = iota((nb, 4 * nf), 1)
    pick = iota((nb, 4 * nf), 0) == (col // nf) * ni + lax.rem(col, ni)
    wide = jnp.dot(
        lji[...].reshape(na * nk, nb), pick.astype(f32).astype(bf16), preferred_element_type=f32)
    same = iota((na * nk, 4 * nf), 0) // nk == lax.rem(iota((na * nk, 4 * nf), 1), nf) // ni
    lbig[...] = jnp.where(same, wide, 0.0).astype(bf16)

    own.wait()
    for cp in exchange:
        cp.wait()

    peers = (across, diag, partner)

    def mix_copy(i):
        return pltpu.make_async_remote_copy(
            mix_s.at[peers[i]], routed.at[f], mix_send.at[i], mix_recv.at[i],
            device_id={"fsdp": peers[i]}, device_id_type=MESH)

    mixed = lax.dot_general(
        spread[...].reshape(N, features), rbig[...], (((1,), (1,)), ((), ())),
        preferred_element_type=f32).astype(bf16)
    for g in range(4):
        mix_s[g] = mixed[:, g * nf:(g + 1) * nf]
    for i in range(3):
        mix_copy(i).start()
    routed[f] = mix_s[f]

    def send_a(t):
        return pltpu.make_async_remote_copy(
            pbuf.at[t, 1 - c], recv_a.at[t], a_send.at[t], a_recv.at[t],
            device_id={"fsdp": partner}, device_id_type=MESH)

    def send_b(t):
        return pltpu.make_async_remote_copy(
            sbuf.at[t, 1 - x], recv_b.at[t], b_send.at[t], b_recv.at[t],
            device_id={"fsdp": across}, device_id_type=MESH)

    def send_hx(t):
        return pltpu.make_async_remote_copy(
            hid.at[t, q], hid.at[t, q], hx_send.at[t], hx_recv.at[t],
            device_id={"fsdp": across}, device_id_type=MESH)

    def send_hp(t):
        return pltpu.make_async_remote_copy(
            hid.at[t, q], hid.at[t, q], hp_send.at[t], hp_recv.at[t],
            device_id={"fsdp": partner}, device_id_type=MESH)

    def send_r(t):
        return pltpu.make_async_remote_copy(
            hid.at[t, q_across], hid.at[t, q_across], r_send.at[t], r_recv.at[t],
            device_id={"fsdp": partner}, device_id_type=MESH)

    def step(t, carry):
        @pl.when(t < n)
        def _():
            @pl.when(t + 1 < n)
            def _():
                for cp in weights(t + 1):
                    cp.start()

            for cp in weights(t):
                cp.wait()
            s = lax.rem(t, 2)
            toks = spread[...].reshape(4 * rows, features)
            for k, w in ((0, wg), (1, wu)):
                part = jnp.dot(toks, w[s], preferred_element_type=f32).astype(bf16)
                for h in range(2):
                    pbuf[t, h, k] = part[h * 2 * rows:(h + 1) * 2 * rows]
            send_a(t).start()

        @pl.when(t >= 3)
        def _():
            u = t - 3

            @pl.when(u + 1 < n)
            def _():
                down(u + 1).start()

            down(u).wait()
            send_hp(u).wait_recv()
            send_r(u).wait_recv()
            s = lax.rem(u, 2)
            h = hid[u].reshape(4 * rows, width)

            @pl.loop(0, T)
            def _(b):
                cc = pl.ds(pl.multiple_of(b * cols, cols), cols)
                acc[b] += jnp.dot(h, wd[s, :, cc], preferred_element_type=f32)

        @pl.when(t < n)
        def _():
            send_a(t).wait_recv()
            for k in range(2):
                total = pbuf[t, c, k].astype(f32) + recv_a[t, k].astype(f32)
                total = total.astype(bf16)
                for h in range(2):
                    sbuf[t, h, k] = total[h * rows:(h + 1) * rows]
            send_b(t).start()

        @pl.when((t >= 1) & (t < n + 1))
        def _():
            u = t - 1
            send_b(u).wait_recv()
            gate = sbuf[u, x, 0].astype(f32) + recv_b[u, 0].astype(f32)
            up = sbuf[u, x, 1].astype(f32) + recv_b[u, 1].astype(f32)
            hid[u, q] = (jax.nn.silu(gate) * up).astype(bf16)
            send_hx(u).start()
            send_hp(u).start()

        @pl.when(t == 2)
        def _():
            for i in range(3):
                mix_copy(i).wait_recv()
            total = jnp.zeros((N, na * nk), f32)
            for g in range(4):
                total += lax.dot_general(
                    routed[g], lbig[:, g * nf:(g + 1) * nf], (((1,), (1,)), ((), ())),
                    preferred_element_type=f32)
            student[...] = total

        @pl.when((t >= 2) & (t < n + 2))
        def _():
            u = t - 2
            send_hx(u).wait_recv()
            send_r(u).start()

        return carry

    lax.fori_loop(0, n + 3, step, 0)

    piece = 4 * rows // PIECES

    def send_right(d, s):
        return pltpu.make_async_remote_copy(
            send_z.at[0, d, s], recv_z.at[0, d, s], z_send.at[0, d, s], z_recv.at[0, d, s],
            device_id={"tensor": z + 1}, device_id_type=MESH)

    def send_left(d, s):
        return pltpu.make_async_remote_copy(
            send_z.at[1, d, s], recv_z.at[1, d, s], z_send.at[1, d, s], z_recv.at[1, d, s],
            device_id={"tensor": z - 1}, device_id_type=MESH)

    def hop(way, d, s, has_prev, sender):
        rr = slice(s * piece, (s + 1) * piece)
        mine = acc[d, rr].astype(bf16)
        send_z[way, d, s] = mine

        @pl.when(has_prev)
        def _():
            sender(d, s).wait_recv()
            send_z[way, d, s] = (mine.astype(f32) + recv_z[way, d, s].astype(f32)).astype(bf16)

        sender(d, s).start()

    for j in range(T - 1):
        for s in range(PIECES):
            dr, dl = T - 1 - j, j

            @pl.when(z < dr)
            def _():
                hop(0, dr, s, z > 0, send_right)

            @pl.when(z > dl)
            def _():
                hop(1, dl, s, z < T - 1, send_left)

    for s in range(PIECES):
        rr = slice(s * piece, (s + 1) * piece)
        tgt[rr] = acc[z, rr].astype(bf16).astype(f32)

        @pl.when(z > 0)
        def _():
            send_right(z, s).wait_recv()
            tgt[rr] += recv_z[0, z, s].astype(f32)

        @pl.when(z < T - 1)
        def _():
            send_left(z, s).wait_recv()
            tgt[rr] += recv_z[1, z, s].astype(f32)

    def mg_copy(i):
        return pltpu.make_async_remote_copy(
            mg_s.at[peers[i]], mg_r.at[f], mg_send.at[i], mg_recv.at[i],
            device_id={"fsdp": peers[i]}, device_id_type=MESH)

    def gl_copy(d):
        peer = lax.rem(z + d, T)
        return pltpu.make_async_remote_copy(
            gl_s.at[:, peer], gl_out.at[pl.ds(z * na, na)], gl_send.at[d], gl_recv.at[d],
            device_id={"tensor": peer}, device_id_type=MESH)

    def gr_copy(g):
        return pltpu.make_async_remote_copy(
            gr_s.at[g], gr_out.at[z], gr_send.at[g], gr_recv.at[z],
            device_id={"tensor": g}, device_id_type=MESH)

    out_grad = (student[...] - tgt[...]) * (1.0 / math.sqrt(N))
    narrow = out_grad.astype(bf16)
    mixed_grad = jnp.dot(narrow, lbig[...], preferred_element_type=f32).astype(bf16)
    for g in range(4):
        mg_s[g] = mixed_grad[:, g * nf:(g + 1) * nf]
    for i in range(3):
        mg_copy(i).start()
    mg_r[f] = mg_s[f]

    turned = out_grad.T.astype(bf16)
    keep = iota((na * nk, nf), 0) // nk == iota((na * nk, nf), 1) // ni
    total = jnp.zeros((na * nk, nb), f32)
    for g in range(4):
        part = jnp.dot(turned, routed[g], preferred_element_type=f32)
        fold = iota((nf, nb), 1) == g * ni + lax.rem(iota((nf, nb), 0), ni)
        total += jnp.dot(
            jnp.where(keep, part, 0.0), fold.astype(f32),
            precision=lax.Precision.HIGHEST, preferred_element_type=f32)
    gl_s[...] = total.reshape(na, T, nk // T, nb)
    for d in range(1, T):
        gl_copy(d).start()
    gl_out[pl.ds(z * na, na)] = gl_s[:, z]

    row_block = lax.rem(iota((nf, nj), 0), ni)

    def grad_right(g):
        flipped = mg_r[g].astype(f32).T.astype(bf16)
        total = jnp.zeros((nf, nj), f32)
        for i in range(0, ni, 2):
            rhs = spread[:, :, i * nj:(i + 2) * nj].reshape(N, 2 * nj)
            part = jnp.dot(flipped, rhs, preferred_element_type=f32)
            for k in range(2):
                total += jnp.where(row_block == i + k, part[:, k * nj:(k + 1) * nj], 0.0)
        gr_s[g] = total.reshape(na, ni, nj)

        @pl.when(g != z)
        def _():
            gr_copy(g).start()

        @pl.when(g == z)
        def _():
            gr_out[z] = gr_s[g]

    grad_right(f)
    for i in (2, 0, 1):
        mg_copy(i).wait_recv()
        grad_right(peers[i])

    for d in range(1, T):
        gl_copy(d).wait()
    for g in range(T):
        @pl.when(z != g)
        def _():
            gr_copy(g).wait_send()
            pltpu.make_async_remote_copy(
                gr_s.at[g], gr_out.at[g], gr_send.at[g], gr_recv.at[g],
                device_id={"tensor": g}, device_id_type=MESH).wait_recv()

    for i in range(3):
        mix_copy(i).wait_send()
        mg_copy(i).wait_send()

    for j in range(T - 1):
        for s in range(PIECES):
            dr, dl = T - 1 - j, j

            @pl.when(z < dr)
            def _():
                send_right(dr, s).wait_send()

            @pl.when(z > dl)
            def _():
                send_left(dl, s).wait_send()

    def drain(t, carry):
        for sender in (send_a, send_b, send_hx, send_hp, send_r):
            sender(t).wait_send()
        return carry

    lax.fori_loop(0, n, drain, 0)


def fused_body(tokens, gate_weight, up_weight, down_weight, right_factor, left_factor):
    T = lax.axis_size("tensor")
    right = jnp.transpose(right_factor, (1, 0, 2))
    rows = tokens.shape[0]
    features, hidden = gate_weight.shape
    width = CHUNK
    n = hidden // width
    cols = down_weight.shape[1] // T
    bf16, f32 = jnp.bfloat16, jnp.float32
    dma = pltpu.SemaphoreType.DMA
    anyspace = pl.BlockSpec(memory_space=pl.ANY)
    vmem = pl.BlockSpec(memory_space=pltpu.VMEM)
    ni, nkr, nj = right_factor.shape
    na, nkl, nb = left_factor.shape[0] // T, left_factor.shape[1], left_factor.shape[2]
    nf, nk = na * ni, nkl * T
    grad_right, grad_left = pl.pallas_call(
        functools.partial(layer_kernel, n, T, rows, width, cols),
        out_shape=(
            jax.ShapeDtypeStruct((T, na, ni, nj), f32),
            jax.ShapeDtypeStruct((T * na, nkl, nb), f32),
        ),
        in_specs=[anyspace] * 6,
        out_specs=(vmem, vmem),
        scratch_shapes=[
            pltpu.VMEM((2, features, width), bf16),
            pltpu.VMEM((2, features, width), bf16),
            pltpu.VMEM((2, width, T * cols), bf16),
            pltpu.VMEM((n, 2, 2, 2 * rows, width), bf16),
            pltpu.VMEM((n, 2, 2 * rows, width), bf16),
            pltpu.VMEM((n, 2, 2, rows, width), bf16),
            pltpu.VMEM((n, 2, rows, width), bf16),
            pltpu.VMEM((n, 4, rows, width), bf16),
            pltpu.VMEM((T, 4 * rows, cols), f32),
            pltpu.VMEM((2, T, PIECES, 4 * rows // PIECES, cols), bf16),
            pltpu.VMEM((2, T, PIECES, 4 * rows // PIECES, cols), bf16),
            pltpu.VMEM((4, rows, features), bf16),
            pltpu.VMEM((4 * rows, cols), f32),
            pltpu.VMEM((T, na, ni, nj), bf16),
            pltpu.VMEM((na, T, nkl, nb), bf16),
            pltpu.VMEM((4 * nf, features), bf16),
            pltpu.VMEM((na * nk, 4 * nf), bf16),
            pltpu.VMEM((4, 4 * rows, nf), bf16),
            pltpu.VMEM((4, 4 * rows, nf), bf16),
            pltpu.VMEM((4 * rows, na * nk), f32),
            pltpu.VMEM((4, 4 * rows, nf), bf16),
            pltpu.VMEM((4, 4 * rows, nf), bf16),
            pltpu.VMEM((4, na, ni, nj), f32),
            pltpu.VMEM((na, T, nkl, nb), f32),
            dma((4,)), dma((3,)), dma((3, 2)),
            dma((n,)), dma((n,)), dma((n,)), dma((n,)),
            dma((n,)), dma((n,)), dma((n,)), dma((n,)), dma((n,)), dma((n,)),
            dma((2, T, PIECES)), dma((2, T, PIECES)),
            dma((T,)), dma((T,)), dma((T,)), dma((T,)),
            dma((3,)), dma((3,)), dma((3,)), dma((3,)),
            dma((T,)), dma((T,)), dma((T,)), dma((T,)),
        ],
        compiler_params=pltpu.CompilerParams(
            collective_id=0, has_side_effects=True, vmem_limit_bytes=62 * 1024 * 1024
        ),
        name="layer",
    )(tokens, gate_weight, up_weight, down_weight, right, left_factor)
    grad_right = jnp.transpose(grad_right.reshape(T * na, ni, nj), (1, 0, 2))
    return (grad_right, grad_left)


def body(tokens, gate_weight, up_weight, down_weight, right_factor, left_factor):
    F, T = lax.axis_size("fsdp"), lax.axis_size("tensor")
    fits = (
        F == 4
        and T == 4
        and gate_weight.shape[1] % CHUNK == 0
        and left_factor.shape[0] % T == 0
        and right_factor.shape[1] % T == 0
        and gate_weight.shape[0] <= 2048
        and tokens.shape[0] == 128
    )
    run = fused_body if fits else plain_body
    return run(tokens, gate_weight, up_weight, down_weight, right_factor, left_factor)


def solution(mesh):
    return jax.shard_map(
        body,
        mesh=mesh,
        in_specs=(
            P(("groups", "fsdp"), None),
            P("fsdp", "tensor"),
            P("fsdp", "tensor"),
            P("tensor", "fsdp"),
            P("fsdp", "tensor", None),
            P("fsdp", "tensor", None),
        ),
        out_specs=(P(("groups", "fsdp"), "tensor", None), P(("groups", "fsdp"), "tensor", None)),
        check_vma=False,
    )
```
